32 devices in a mesh: tile: 8 (over z, x), mem: 4 (over y, core).
Axes of the slice: x: 2, y: 2, z: 4, core: 2. Of those that a mesh axis runs over, the one named last changes fastest.
Arguments:
- prior_ensemble_fields: float32 [128, 32, 512], P('mem', 'tile'), may hold values from -6 to 6
- vel_y: float32 [32, 512], P('tile'), may hold values from -0.4 to 0.4
- vel_x: float32 [32, 512], P('tile'), may hold values from -0.4 to 0.4
- diffus: float32 [32, 512], P('tile'), may hold values from 0.02 to 0.2
- assign: int32 [8, 2048], P('tile'), may hold values from 0 to 2047, each once within a row
- obs_cell: int32 [64, 512], P(('tile', 'mem')), may hold values from 0 to 255
- obs_value: float32 [64, 512], P(('tile', 'mem')), may hold values from -6 to 6
- obs_var: float32 [64, 512], P(('tile', 'mem')), may hold values from 0.2 to 2
Outputs:
- analysis: float32 [128, 32, 512], P('mem', 'tile')
The draws below stay inside these ranges and needn't reach their ends.
All inputs are finite; a program needn't handle non-finite values.
Results may differ from the reference program's by a relative error of at most 0.0003.
Values sent between devices are 32-bit elements; how exact they have to be, the bound alone decides.
A program may use at most 64 MiB of HBM per device.

```python
import math
import jax
import jax.numpy as jnp
from jax import lax

WIDTH = 512
PANEL_HEIGHT = 4
PATCH = 256
NOBS = 512
ENS = 128
PANEL_WIDTH_GRID = 2048
NY = 32
PATCHES = 64
N_TILE = 8


def set_ends(values, key, low, high):
    extent = values.shape
    index_at = [jax.random.randint(jax.random.fold_in(key, axis), (), 0, extent[axis]) for axis in range(len(extent))]
    values = values.at[tuple(index_at)].set(low)
    longest = extent.index(max(extent))
    index_at[longest] = (index_at[longest] + 1) % extent[longest]
    return values.at[tuple(index_at)].set(high)


def level_of(rng, dims, cuts, low, largest):
    loudness = 1.0
    for dim, shards_of in cuts:
        draws = jax.random.uniform(jax.random.fold_in(jax.random.fold_in(rng, 6), dim), (shards_of,), jnp.float32, low / len(cuts), largest / len(cuts))
        loudness = loudness * jnp.repeat(jnp.exp(draws), dims[dim] // shards_of).reshape((-1,) + (1,) * (len(dims) - 1 - dim))
    return loudness


def scatter_about(own_key, shape, scale, bound, pieces=(), held_as=jnp.bfloat16):
    result = scale * jax.random.normal(own_key, shape, jnp.float32)
    if pieces:
        result = result * level_of(own_key, shape, pieces, -0.22, 0.18)
    return jnp.clip(result, -bound, bound).astype(held_as)


def setup_inputs(seed: int = 0) -> dict:
    seeds = jax.random.split(jax.random.key(seed), 9)
    prior_ensemble_fields = scatter_about(seeds[0], (ENS, NY, WIDTH), 1.0, 6.0, ((0, 4), (1, 8)), jnp.float32)
    vel_y = jnp.clip(jax.random.uniform(seeds[1], (NY, WIDTH), jnp.float32, -0.4, 0.4) * level_of(seeds[1], (NY, WIDTH), ((0, 8),), -0.4, 0.0), -0.4, 0.4)
    vel_x = jnp.clip(jax.random.uniform(seeds[2], (NY, WIDTH), jnp.float32, -0.4, 0.4) * level_of(seeds[2], (NY, WIDTH), ((0, 8),), -0.4, 0.0), -0.4, 0.4)
    diffus = jnp.clip(jnp.exp(math.log(0.2) - 2.3025851 * jax.random.uniform(seeds[3], (NY, WIDTH), jnp.float32) ** level_of(seeds[3], (NY, WIDTH), ((0, 8),), -0.2, 0.2)), 0.02, 0.2)
    assign = jax.vmap(lambda own: jax.random.permutation(own, PANEL_WIDTH_GRID))(jax.random.split(seeds[4], N_TILE)).reshape((N_TILE, PANEL_WIDTH_GRID)).astype(jnp.int32)
    obs_cell = set_ends(jax.random.randint(seeds[5], (PATCHES, NOBS), 0, PATCH), jax.random.fold_in(seeds[5], 1), 0, PATCH - 1).astype(jnp.int32)
    obs_value = scatter_about(seeds[6], (PATCHES, NOBS), 1.0, 6.0, ((0, 32),), jnp.float32)
    obs_var = jnp.clip(jnp.exp(math.log(2.0) - 2.3025851 * jax.random.uniform(seeds[7], (PATCHES, NOBS), jnp.float32) ** level_of(seeds[7], (PATCHES, NOBS), ((0, 32),), -0.2, 0.2)), 0.2, 2.0)
    return dict(prior_ensemble_fields=prior_ensemble_fields, vel_y=vel_y, vel_x=vel_x, diffus=diffus, assign=assign, obs_cell=obs_cell, obs_value=obs_value, obs_var=obs_var)


def advance(padded, coef_y, coef_x, coef_k):
    center = padded[..., 2:-2, :]
    above = padded[..., 3:-1, :]
    below = padded[..., 1:-3, :]
    grad_y = (-padded[..., 4:, :] + 8.0 * above - 8.0 * below + padded[..., :-4, :]) / 12.0
    lap_y = above - 2.0 * center + below
    right_one = jnp.roll(center, -1, axis=-1)
    left_one = jnp.roll(center, 1, axis=-1)
    grad_x = (-jnp.roll(center, -2, axis=-1) + 8.0 * right_one - 8.0 * left_one + jnp.roll(center, 2, axis=-1)) / 12.0
    lap_x = right_one - 2.0 * center + left_one
    return center - coef_y * grad_y - coef_x * grad_x + coef_k * (lap_y + lap_x)

def analyze(members, cells, observed, variance):
    ensemble_size = members.shape[0]
    highest = lax.Precision.HIGHEST
    center = jnp.mean(members, axis=0)
    spread = members - center[None, :]
    obs_spread = jnp.take(spread, cells, axis=1)
    innovation = observed - jnp.take(center, cells)
    weighted = obs_spread / variance[None, :]
    gram = jnp.dot(weighted.astype(jnp.float32), obs_spread.T.astype(jnp.float32), precision=highest, preferred_element_type=jnp.float32)
    system = gram + (ensemble_size - 1.0) * jnp.eye(ensemble_size, dtype=jnp.float32)
    factor = jnp.linalg.cholesky(system)
    pulled = jnp.dot(weighted.astype(jnp.float32), innovation.astype(jnp.float32), precision=highest, preferred_element_type=jnp.float32)
    right_side = jnp.concatenate([pulled[:, None], gram], axis=1)
    solved = jax.scipy.linalg.cho_solve((factor, True), right_side)
    gain_mean = solved[:, 0]
    mixing = solved[:, 1:]
    transform = jnp.eye(ensemble_size, dtype=jnp.float32) - 0.5 * mixing + gain_mean[None, :]
    return center[None, :] + jnp.dot(transform.astype(jnp.float32), spread.astype(jnp.float32), precision=highest, preferred_element_type=jnp.float32)

def reference(prior_ensemble_fields, vel_y, vel_x, diffus, assign, obs_cell, obs_value, obs_var):
    ensemble_size = prior_ensemble_fields.shape[0]
    per_tile = PANEL_WIDTH_GRID // PATCH

    def one_step(member):
        return advance(jnp.pad(member, ((2, 2), (0, 0))), vel_y, vel_x, diffus)

    def paired_advance_update(member):
        return one_step(one_step(member))
    predict_advance = lax.map(paired_advance_update, prior_ensemble_fields)

    def tile_update(panel_number):
        panel_entries = lax.dynamic_slice_in_dim(predict_advance, (panel_number * PANEL_HEIGHT).astype(jnp.int32), PANEL_HEIGHT, 1).reshape(ensemble_size, PANEL_WIDTH_GRID)
        order = assign[panel_number]
        permuted = jnp.take(panel_entries, order, axis=1).reshape(ensemble_size, per_tile, PATCH)
        first = (panel_number * per_tile).astype(jnp.int32)
        cells = lax.dynamic_slice_in_dim(obs_cell, first, per_tile, 0)
        values = lax.dynamic_slice_in_dim(obs_value, first, per_tile, 0)
        variances = lax.dynamic_slice_in_dim(obs_var, first, per_tile, 0)
        updated = jax.vmap(analyze, in_axes=(1, 0, 0, 0), out_axes=1)(permuted, cells, values, variances)
        updated = updated.reshape(ensemble_size, PANEL_WIDTH_GRID)
        positions = jnp.argsort(order).astype(jnp.int32)
        return jnp.take(updated, positions, axis=1).reshape(ensemble_size, PANEL_HEIGHT, WIDTH)
    tiles = lax.map(tile_update, jnp.arange(N_TILE, dtype=jnp.int32))
    analysed = jnp.transpose(tiles, (1, 0, 2, 3)).reshape(ensemble_size, NY, WIDTH)
    return lax.map(one_step, analysed)
```

```python
import jax
import jax.numpy as jnp
from jax import lax
from jax.experimental import pallas as pl
from jax.experimental.pallas import tpu as pltpu
from jax.sharding import PartitionSpec as P

PATCH = 256


def extended(block, sides, width):
    for axis, dim in sides:
        count = lax.axis_size(axis)
        forward = [(i, i + 1) for i in range(count - 1)]
        backward = [(target, source) for source, target in forward]
        low = lax.ppermute(
            lax.slice_in_dim(block, block.shape[dim] - width, None, axis=dim), axis, forward
        )
        high = lax.ppermute(lax.slice_in_dim(block, 0, width, axis=dim), axis, backward)
        block = jnp.concatenate([low, block, high], axis=dim)
    return block


def advance(padded, coef_y, coef_x, coef_k):
    center = padded[..., 2:-2, :]
    above = padded[..., 3:-1, :]
    below = padded[..., 1:-3, :]
    grad_y = (-padded[..., 4:, :] + 8.0 * above - 8.0 * below + padded[..., :-4, :]) / 12.0
    lap_y = above - 2.0 * center + below
    right_one = jnp.roll(center, -1, axis=-1)
    left_one = jnp.roll(center, 1, axis=-1)
    grad_x = (
        -jnp.roll(center, -2, axis=-1)
        + 8.0 * right_one
        - 8.0 * left_one
        + jnp.roll(center, 2, axis=-1)
    ) / 12.0
    lap_x = right_one - 2.0 * center + left_one
    return center - coef_y * grad_y - coef_x * grad_x + coef_k * (lap_y + lap_x)


def dot(a, b, dims=(((1,), (0,)), ((), ()))):
    return lax.dot_general(
        a, b, dims, precision=lax.Precision.HIGHEST, preferred_element_type=jnp.float32
    )


NT = (((1,), (1,)), ((), ()))


def analysis_kernel(members_ref, cells_ref, observed_ref, variance_ref, out_ref, system_ref, inverse_ref):
    size = members_ref.shape[0]
    patches = cells_ref.shape[0]
    floor = size - 1.0
    eye = jnp.where(
        lax.broadcasted_iota(jnp.int32, (size, size), 0)
        == lax.broadcasted_iota(jnp.int32, (size, size), 1),
        1.0,
        0.0,
    )
    spreads, centers, pulls, excess = [], [], [], []
    for p in range(patches):
        x = members_ref[:, p * PATCH : (p + 1) * PATCH]
        center = jnp.mean(x, axis=0, keepdims=True)
        spread = x - center
        cells = cells_ref[p : p + 1, :]
        nobs = cells.shape[1]
        hot = jnp.where(
            lax.broadcasted_iota(jnp.int32, (PATCH, nobs), 0) == cells, 1.0, 0.0
        )
        inverse_var = 1.0 / variance_ref[p : p + 1, :]
        pair = jnp.concatenate(
            [inverse_var, observed_ref[p : p + 1, :] * inverse_var, jnp.zeros((6, nobs), jnp.float32)],
            axis=0,
        )
        sums = dot(pair, hot, NT)
        d, w = sums[0:1], sums[1:2]
        gram = dot(spread * d, spread, NT)
        pulled = dot(jnp.broadcast_to(w - d * center, (8, PATCH)), spread, NT)
        bound = jnp.max(jnp.sum(jnp.abs(gram), axis=0, keepdims=True)) * 1.0001
        system = gram + floor * eye
        system_ref[p] = system
        scale = 2.0 / (2.0 * floor + bound)
        inverse_ref[p] = (2.0 * scale) * eye - (scale * scale) * system
        e = bound / floor
        spreads.append(spread)
        centers.append(center)
        pulls.append(pulled)
        excess.append(e * e / (4.0 * (1.0 + e)))

    def more(es):
        worst = es[0]
        for e in es[1:]:
            worst = jnp.maximum(worst, e)
        return worst > 1e-6

    def step(es):
        xs = [inverse_ref[p] for p in range(patches)]
        ms = [dot(xs[p], system_ref[p]) for p in range(patches)]
        ys = [dot(ms[p], xs[p]) for p in range(patches)]
        for p in range(patches):
            s = 2.0 * (1.0 + es[p]) / (2.0 + es[p])
            inverse_ref[p] = (2.0 * s) * xs[p] - (s * s) * ys[p]
        return tuple(e * e / (4.0 * (1.0 + e)) for e in es)

    lax.while_loop(more, step, tuple(excess))
    for p in range(patches):
        z = dot(inverse_ref[p], spreads[p])
        shift = dot(pulls[p], z)[0:1]
        out_ref[:, p * PATCH : (p + 1) * PATCH] = (
            centers[p] + shift + 0.5 * spreads[p] + (0.5 * floor) * z
        )


def analyze(members, cells, observed, variance):
    size = members.shape[0]
    patches = cells.shape[0]
    return pl.pallas_call(
        analysis_kernel,
        out_shape=jax.ShapeDtypeStruct(members.shape, jnp.float32),
        in_specs=[pl.BlockSpec(memory_space=pltpu.VMEM)] * 4,
        out_specs=pl.BlockSpec(memory_space=pltpu.VMEM),
        scratch_shapes=[
            pltpu.VMEM((patches, size, size), jnp.float32),
            pltpu.VMEM((patches, size, size), jnp.float32),
        ],
    )(members, cells, observed, variance)


def on_device(prior_ensemble_fields, vel_y, vel_x, diffus, assign, obs_cell, obs_value, obs_var):
    local_members, tile_rows, width_cells = prior_ensemble_fields.shape
    columns = tile_rows * width_cells
    groups = lax.axis_size("mem")
    group_columns = columns // groups
    ensemble = prior_ensemble_fields
    stacked = jnp.concatenate([ensemble, vel_y[None], vel_x[None], diffus[None]], axis=0)
    widened = extended(stacked, (("tile", 1),), 4)
    field_rows = widened[:local_members]
    near_y = widened[local_members, 2:-2]
    near_x = widened[local_members + 1, 2:-2]
    near_k = widened[local_members + 2, 2:-2]
    middle = advance(field_rows, near_y, near_x, near_k)
    first_row = lax.axis_index("tile") * tile_rows - 2
    global_rows = first_row + jnp.arange(tile_rows + 4, dtype=jnp.int32)
    inside = (global_rows >= 0) & (global_rows < tile_rows * lax.axis_size("tile"))
    middle = jnp.where(inside[None, :, None], middle, 0.0)
    ensemble = advance(middle, vel_y, vel_x, diffus)
    order = assign[0]
    permuted = jnp.take(ensemble.reshape(local_members, columns), order, axis=1)
    blocks = permuted.reshape(local_members, groups, group_columns)
    gathered = lax.all_to_all(blocks, "mem", split_axis=1, concat_axis=0, tiled=True)
    updated = analyze(
        gathered.reshape(local_members * groups, group_columns), obs_cell, obs_value, obs_var
    )
    outgoing = updated.reshape(local_members * groups, 1, group_columns)
    returned = lax.all_to_all(outgoing, "mem", split_axis=0, concat_axis=1, tiled=True)
    returned = returned.reshape(local_members, columns)
    positions = jnp.argsort(order)
    analysed = jnp.take(returned, positions, axis=1).reshape(local_members, tile_rows, width_cells)
    padded = extended(analysed, (("tile", 1),), 2)
    return advance(padded, vel_y, vel_x, diffus)


def solution(mesh):
    return jax.shard_map(
        on_device,
        mesh=mesh,
        in_specs=(
            P("mem", "tile", None),
            P("tile", None),
            P("tile", None),
            P("tile", None),
            P("tile", None),
            P(("tile", "mem"), None),
            P(("tile", "mem"), None),
            P(("tile", "mem"), None),
        ),
        out_specs=P("mem", "tile", None),
        check_vma=False,
    )
```

```python
import functools

import jax
import jax.numpy as jnp
from jax import lax
from jax.experimental import pallas as pl
from jax.experimental.pallas import tpu as pltpu
from jax.sharding import PartitionSpec as P

PATCH = 256


MESH = pl.DeviceIdType.MESH
NN = (((1,), (0,)), ((), ()))


def one_step(rows, coef_y, coef_x, coef_k):
    far_below, below, center, above, far_above = rows
    width = center.shape[1]
    grad_y = (far_below - far_above + 8.0 * (above - below)) * (1.0 / 12.0)
    right_one = pltpu.roll(center, width - 1, 1)
    left_one = pltpu.roll(center, 1, 1)
    right_two = pltpu.roll(center, width - 2, 1)
    left_two = pltpu.roll(center, 2, 1)
    grad_x = (left_two - right_two + 8.0 * (right_one - left_one)) * (1.0 / 12.0)
    lap = (above + below) + (right_one + left_one) - 4.0 * center
    return center - coef_y * grad_y - coef_x * grad_x + coef_k * lap


def enter(tile, tiles, me, groups):
    barrier = pltpu.get_barrier_semaphore()
    for k in range(1, groups):
        pl.semaphore_signal(
            barrier, inc=1, device_id={"mem": lax.rem(me + k, groups)}, device_id_type=MESH
        )

    @pl.when(tile > 0)
    def _():
        pl.semaphore_signal(barrier, inc=1, device_id={"tile": tile - 1}, device_id_type=MESH)

    @pl.when(tile < tiles - 1)
    def _():
        pl.semaphore_signal(barrier, inc=1, device_id={"tile": tile + 1}, device_id_type=MESH)

    edges = jnp.where(tile > 0, 1, 0) + jnp.where(tile < tiles - 1, 1, 0)
    pl.semaphore_wait(barrier, groups - 1 + edges)


def build_hot(order_ref, hot_ref):
    columns = hot_ref.shape[0]
    block = 128

    def fill(i, carry):
        start = pl.multiple_of(i * block, block)
        row = lax.broadcasted_iota(jnp.int32, (block, columns), 0) + start
        hot_ref[pl.ds(start, block), :] = jnp.where(row == order_ref[...], 1.0, 0.0).astype(
            jnp.bfloat16
        )
        return carry

    lax.fori_loop(0, columns // block, fill, 0)


def split_into(parts_ref, value, start):
    rows, width = value.shape
    high = value.astype(jnp.bfloat16)
    rest = value - high.astype(jnp.float32)
    middle = rest.astype(jnp.bfloat16)
    low = (rest - middle.astype(jnp.float32)).astype(jnp.bfloat16)
    for i, part in enumerate((high, middle, low)):
        parts_ref[i * rows : (i + 1) * rows, start : start + width] = part


def picked(parts_ref, hot, dims):
    wide = lax.dot_general(parts_ref[...], hot, dims, preferred_element_type=jnp.float32)
    rows = wide.shape[0] // 3
    return wide[:rows] + (wide[rows : 2 * rows] + wide[2 * rows :])


def forecast_kernel(
    tiles, groups, prior_ref, vy_ref, vx_ref, dk_ref, order_ref, out_ref,
    below_ref, above_ref, below_c, above_c, hot_ref, parts_ref, outgoing, incoming,
    up_send, up_recv, down_send, down_recv, mem_send, mem_recv,
):
    tile, me = lax.axis_index("tile"), lax.axis_index("mem")
    members, height, width = prior_ref.shape
    group_columns = out_ref.shape[1]
    has_below, has_above = tile > 0, tile < tiles - 1
    enter(tile, tiles, me, groups)

    def halo(target, field, coefs, send, recv):
        pairs = [(prior_ref, field)] + [
            (ref, coefs.at[i]) for i, ref in enumerate((vy_ref, vx_ref, dk_ref))
        ]
        return [
            pltpu.make_async_remote_copy(
                src_ref=src, dst_ref=dst, send_sem=send.at[i], recv_sem=recv.at[i],
                device_id={"tile": target}, device_id_type=MESH,
            )
            for i, (src, dst) in enumerate(pairs)
        ]

    up = halo(tile + 1, below_ref, below_c, up_send, up_recv)
    down = halo(tile - 1, above_ref, above_c, down_send, down_recv)

    @pl.when(has_above)
    def _():
        for c in up:
            c.start()

    @pl.when(has_below)
    def _():
        for c in down:
            c.start()

    @pl.when(jnp.logical_not(has_below))
    def _():
        below_ref[...] = jnp.zeros_like(below_ref)
        below_c[...] = jnp.zeros_like(below_c)

    @pl.when(jnp.logical_not(has_above))
    def _():
        above_ref[...] = jnp.zeros_like(above_ref)
        above_c[...] = jnp.zeros_like(above_c)

    build_hot(order_ref, hot_ref)

    @pl.when(has_below)
    def _():
        for c in up:
            c.wait_recv()

    @pl.when(has_above)
    def _():
        for c in down:
            c.wait_recv()

    def slab(r):
        if r < 0:
            return below_ref[:, height + r, :]
        if r >= height:
            return above_ref[:, r - height, :]
        return prior_ref[:, r, :]

    def coefs(r):
        if r < 0:
            return [below_c[i, height + r : height + r + 1, :] for i in range(3)]
        if r >= height:
            return [above_c[i, r - height : r - height + 1, :] for i in range(3)]
        return [ref[r : r + 1, :] for ref in (vy_ref, vx_ref, dk_ref)]

    keep_below = jnp.where(has_below, 1.0, 0.0)
    keep_above = jnp.where(has_above, 1.0, 0.0)
    middle = {}
    for r in range(-2, height + 2):
        value = one_step([slab(r + o) for o in range(-2, 3)], *coefs(r))
        if r < 0:
            value = value * keep_below
        if r >= height:
            value = value * keep_above
        middle[r] = value
    for r in range(height):
        value = one_step([middle[r + o] for o in range(-2, 3)], *coefs(r))
        split_into(parts_ref, value, r * width)

    sent = []
    order = sorted(range(1, groups), key=lambda k: abs(2 * k - groups))
    for k in order + [0]:
        target = lax.rem(me + k, groups)
        first = pl.multiple_of(target * group_columns, group_columns)
        block = picked(parts_ref, hot_ref[:, pl.ds(first, group_columns)], NN)
        if k == 0:
            out_ref[pl.ds(pl.multiple_of(me * members, members), members), :] = block
            continue
        outgoing[k - 1] = block
        c = pltpu.make_async_remote_copy(
            src_ref=outgoing.at[k - 1], dst_ref=incoming.at[k - 1],
            send_sem=mem_send.at[k - 1], recv_sem=mem_recv.at[k - 1],
            device_id={"mem": target}, device_id_type=MESH,
        )
        c.start()
        sent.append((k, c))
    for k, c in reversed(sent):
        c.wait_recv()
        source = lax.rem(me - k + groups, groups)
        out_ref[pl.ds(pl.multiple_of(source * members, members), members), :] = incoming[k - 1]
    for k, c in sent:
        c.wait_send()

    @pl.when(has_above)
    def _():
        for c in up:
            c.wait_send()

    @pl.when(has_below)
    def _():
        for c in down:
            c.wait_send()


def return_kernel(
    tiles, groups, updated_ref, vy_ref, vx_ref, dk_ref, order_ref, out_ref,
    below_ref, above_ref, rows_ref, hot_ref, incoming, parts_ref, whole_ref,
    up_send, up_recv, down_send, down_recv, mem_send, mem_recv,
):
    tile, me = lax.axis_index("tile"), lax.axis_index("mem")
    members, height, width = out_ref.shape
    group_columns = updated_ref.shape[1]
    has_below, has_above = tile > 0, tile < tiles - 1
    enter(tile, tiles, me, groups)
    sent = []
    for k in sorted(range(1, groups), key=lambda k: abs(2 * k - groups)):
        target = lax.rem(me + k, groups)
        c = pltpu.make_async_remote_copy(
            src_ref=updated_ref.at[pl.ds(pl.multiple_of(target * members, members), members), :],
            dst_ref=incoming.at[k - 1],
            send_sem=mem_send.at[k - 1], recv_sem=mem_recv.at[k - 1],
            device_id={"mem": target}, device_id_type=MESH,
        )
        c.start()
        sent.append((k, c))
    build_hot(order_ref, hot_ref)
    own = pl.multiple_of(me * group_columns, group_columns)
    whole_ref[:, pl.ds(own, group_columns)] = updated_ref[
        pl.ds(pl.multiple_of(me * members, members), members), :
    ]
    for k, c in reversed(sent):
        c.wait_recv()
        source = lax.rem(me - k + groups, groups)
        first = pl.multiple_of(source * group_columns, group_columns)
        whole_ref[:, pl.ds(first, group_columns)] = incoming[k - 1]
    for g in range(groups):
        start = g * group_columns
        split_into(parts_ref, whole_ref[:, start : start + group_columns], start)

    up = pltpu.make_async_remote_copy(
        src_ref=rows_ref.at[pl.ds(height - 2, 2)], dst_ref=below_ref,
        send_sem=up_send, recv_sem=up_recv, device_id={"tile": tile + 1}, device_id_type=MESH,
    )
    down = pltpu.make_async_remote_copy(
        src_ref=rows_ref.at[pl.ds(0, 2)], dst_ref=above_ref,
        send_sem=down_send, recv_sem=down_recv, device_id={"tile": tile - 1}, device_id_type=MESH,
    )
    for r in range(height):
        rows_ref[r] = picked(parts_ref, hot_ref[r * width : (r + 1) * width, :], NT)
        if r == 1:

            @pl.when(has_below)
            def _():
                down.start()

        if r == height - 1:

            @pl.when(has_above)
            def _():
                up.start()

    @pl.when(jnp.logical_not(has_below))
    def _():
        below_ref[...] = jnp.zeros_like(below_ref)

    @pl.when(jnp.logical_not(has_above))
    def _():
        above_ref[...] = jnp.zeros_like(above_ref)

    @pl.when(has_above)
    def _():
        down.wait_recv()

    @pl.when(has_below)
    def _():
        up.wait_recv()

    def slab(r):
        if r < 0:
            return below_ref[2 + r]
        if r >= height:
            return above_ref[r - height]
        return rows_ref[r]

    for r in range(height):
        out_ref[:, r, :] = one_step(
            [slab(r + o) for o in range(-2, 3)],
            *[ref[r : r + 1, :] for ref in (vy_ref, vx_ref, dk_ref)],
        )
    for k, c in sent:
        c.wait_send()

    @pl.when(has_below)
    def _():
        down.wait_send()

    @pl.when(has_above)
    def _():
        up.wait_send()


def dot(a, b, dims=(((1,), (0,)), ((), ()))):
    return lax.dot_general(
        a, b, dims, precision=lax.Precision.HIGHEST, preferred_element_type=jnp.float32
    )


NT = (((1,), (1,)), ((), ()))


def analysis_kernel(members_ref, cells_ref, observed_ref, variance_ref, out_ref, system_ref, inverse_ref):
    size = members_ref.shape[0]
    patches = cells_ref.shape[0]
    floor = size - 1.0
    eye = jnp.where(
        lax.broadcasted_iota(jnp.int32, (size, size), 0)
        == lax.broadcasted_iota(jnp.int32, (size, size), 1),
        1.0,
        0.0,
    )
    spreads, centers, pulls, excess = [], [], [], []
    for p in range(patches):
        x = members_ref[:, p * PATCH : (p + 1) * PATCH]
        center = jnp.mean(x, axis=0, keepdims=True)
        spread = x - center
        cells = cells_ref[p : p + 1, :]
        nobs = cells.shape[1]
        hot = jnp.where(
            lax.broadcasted_iota(jnp.int32, (PATCH, nobs), 0) == cells, 1.0, 0.0
        )
        inverse_var = 1.0 / variance_ref[p : p + 1, :]
        pair = jnp.concatenate(
            [inverse_var, observed_ref[p : p + 1, :] * inverse_var, jnp.zeros((6, nobs), jnp.float32)],
            axis=0,
        )
        sums = dot(pair, hot, NT)
        d, w = sums[0:1], sums[1:2]
        gram = dot(spread * d, spread, NT)
        pulled = dot(jnp.broadcast_to(w - d * center, (8, PATCH)), spread, NT)
        bound = jnp.max(jnp.sum(jnp.abs(gram), axis=0, keepdims=True)) * 1.0001
        system = gram + floor * eye
        system_ref[p] = system
        scale = 2.0 / (2.0 * floor + bound)
        inverse_ref[p] = (2.0 * scale) * eye - (scale * scale) * system
        e = bound / floor
        spreads.append(spread)
        centers.append(center)
        pulls.append(pulled)
        excess.append(e * e / (4.0 * (1.0 + e)))

    def more(es):
        worst = es[0]
        for e in es[1:]:
            worst = jnp.maximum(worst, e)
        return worst > 1e-6

    def step(es):
        xs = [inverse_ref[p] for p in range(patches)]
        ms = [dot(xs[p], system_ref[p]) for p in range(patches)]
        ys = [dot(ms[p], xs[p]) for p in range(patches)]
        for p in range(patches):
            s = 2.0 * (1.0 + es[p]) / (2.0 + es[p])
            inverse_ref[p] = (2.0 * s) * xs[p] - (s * s) * ys[p]
        return tuple(e * e / (4.0 * (1.0 + e)) for e in es)

    lax.while_loop(more, step, tuple(excess))
    for p in range(patches):
        z = dot(inverse_ref[p], spreads[p])
        shift = dot(pulls[p], z)[0:1]
        out_ref[:, p * PATCH : (p + 1) * PATCH] = (
            centers[p] + shift + 0.5 * spreads[p] + (0.5 * floor) * z
        )


def analyze(members, cells, observed, variance):
    size = members.shape[0]
    patches = cells.shape[0]
    return pl.pallas_call(
        analysis_kernel,
        out_shape=jax.ShapeDtypeStruct(members.shape, jnp.float32),
        in_specs=[pl.BlockSpec(memory_space=pltpu.VMEM)] * 4,
        out_specs=pl.BlockSpec(memory_space=pltpu.VMEM),
        scratch_shapes=[
            pltpu.VMEM((patches, size, size), jnp.float32),
            pltpu.VMEM((patches, size, size), jnp.float32),
        ],
    )(members, cells, observed, variance)


def on_device(prior_ensemble_fields, vel_y, vel_x, diffus, assign, obs_cell, obs_value, obs_var):
    members, height, width = prior_ensemble_fields.shape
    columns = height * width
    tiles, groups = lax.axis_size("tile"), lax.axis_size("mem")
    group_columns = columns // groups
    vmem = pl.BlockSpec(memory_space=pltpu.VMEM)
    f32, bf16 = jnp.float32, jnp.bfloat16
    dma = pltpu.SemaphoreType.DMA
    gathered = pl.pallas_call(
        functools.partial(forecast_kernel, tiles, groups),
        out_shape=jax.ShapeDtypeStruct((members * groups, group_columns), f32),
        in_specs=[vmem] * 5,
        out_specs=vmem,
        scratch_shapes=[
            pltpu.VMEM((members, height, width), f32),
            pltpu.VMEM((members, height, width), f32),
            pltpu.VMEM((3, height, width), f32),
            pltpu.VMEM((3, height, width), f32),
            pltpu.VMEM((columns, columns), bf16),
            pltpu.VMEM((3 * members, columns), bf16),
            pltpu.VMEM((groups - 1, members, group_columns), f32),
            pltpu.VMEM((groups - 1, members, group_columns), f32),
            dma((4,)), dma((4,)), dma((4,)), dma((4,)), dma((groups - 1,)), dma((groups - 1,)),
        ],
        compiler_params=pltpu.CompilerParams(collective_id=0, has_side_effects=True),
    )(prior_ensemble_fields, vel_y, vel_x, diffus, assign)
    updated = analyze(gathered, obs_cell, obs_value, obs_var)
    return pl.pallas_call(
        functools.partial(return_kernel, tiles, groups),
        out_shape=jax.ShapeDtypeStruct((members, height, width), f32),
        in_specs=[vmem] * 5,
        out_specs=vmem,
        scratch_shapes=[
            pltpu.VMEM((2, members, width), f32),
            pltpu.VMEM((2, members, width), f32),
            pltpu.VMEM((height, members, width), f32),
            pltpu.VMEM((columns, columns), bf16),
            pltpu.VMEM((groups - 1, members, group_columns), f32),
            pltpu.VMEM((3 * members, columns), bf16),
            pltpu.VMEM((members, columns), f32),
            dma, dma, dma, dma, dma((groups - 1,)), dma((groups - 1,)),
        ],
        compiler_params=pltpu.CompilerParams(collective_id=1, has_side_effects=True),
    )(updated, vel_y, vel_x, diffus, assign)


def solution(mesh):
    return jax.shard_map(
        on_device,
        mesh=mesh,
        in_specs=(
            P("mem", "tile", None),
            P("tile", None),
            P("tile", None),
            P("tile", None),
            P("tile", None),
            P(("tile", "mem"), None),
            P(("tile", "mem"), None),
            P(("tile", "mem"), None),
        ),
        out_specs=P("mem", "tile", None),
        check_vma=False,
    )
```

```python
import functools

import jax
import jax.numpy as jnp
from jax import lax
from jax.experimental import pallas as pl
from jax.experimental.pallas import tpu as pltpu
from jax.sharding import PartitionSpec as P

PATCH = 256


MESH = pl.DeviceIdType.MESH
NN = (((1,), (0,)), ((), ()))


def one_step(rows, coef_y, coef_x, coef_k):
    far_below, below, center, above, far_above = rows
    width = center.shape[1]
    grad_y = (far_below - far_above + 8.0 * (above - below)) * (1.0 / 12.0)
    right_one = pltpu.roll(center, width - 1, 1)
    left_one = pltpu.roll(center, 1, 1)
    right_two = pltpu.roll(center, width - 2, 1)
    left_two = pltpu.roll(center, 2, 1)
    grad_x = (left_two - right_two + 8.0 * (right_one - left_one)) * (1.0 / 12.0)
    lap = (above + below) + (right_one + left_one) - 4.0 * center
    return center - coef_y * grad_y - coef_x * grad_x + coef_k * lap


def enter(tile, tiles, me, groups):
    barrier = pltpu.get_barrier_semaphore()
    for k in range(1, groups):
        pl.semaphore_signal(
            barrier, inc=1, device_id={"mem": lax.rem(me + k, groups)}, device_id_type=MESH
        )

    @pl.when(tile > 0)
    def _():
        pl.semaphore_signal(barrier, inc=1, device_id={"tile": tile - 1}, device_id_type=MESH)

    @pl.when(tile < tiles - 1)
    def _():
        pl.semaphore_signal(barrier, inc=1, device_id={"tile": tile + 1}, device_id_type=MESH)

    edges = jnp.where(tile > 0, 1, 0) + jnp.where(tile < tiles - 1, 1, 0)
    pl.semaphore_wait(barrier, groups - 1 + edges)


def build_hot(order_ref, hot_ref):
    columns = hot_ref.shape[0]
    block = 128

    def fill(i, carry):
        start = pl.multiple_of(i * block, block)
        row = lax.broadcasted_iota(jnp.int32, (block, columns), 0) + start
        hot_ref[pl.ds(start, block), :] = jnp.where(row == order_ref[...], 1.0, 0.0).astype(
            jnp.bfloat16
        )
        return carry

    lax.fori_loop(0, columns // block, fill, 0)


def parts_of(value):
    high = value.astype(jnp.bfloat16)
    low = (value - high.astype(jnp.float32)).astype(jnp.bfloat16)
    return jnp.concatenate([high, low], axis=0)


def picked(parts, hot):
    wide = lax.dot_general(parts, hot, NN, preferred_element_type=jnp.float32)
    rows = wide.shape[0] // 2
    return wide[:rows] + wide[rows:]


def build_inverse_hot(order_ref, hot_ref):
    columns = hot_ref.shape[0]
    block = 128
    across = jnp.concatenate(
        [order_ref[:, i * block : (i + 1) * block] for i in range(columns // block)], axis=0
    )
    across = jnp.concatenate([across] * (block // across.shape[0]), axis=0)
    down = across.T
    place = lax.broadcasted_iota(jnp.int32, (block, columns), 1)
    for i in range(columns // block):
        hot_ref[i * block : (i + 1) * block, :] = jnp.where(
            place == down[:, i : i + 1], 1.0, 0.0
        ).astype(jnp.bfloat16)


def observation_sums(cells_ref, observed_ref, variance_ref, sums_ref):
    patches, nobs = cells_ref.shape
    for p in range(patches):
        hot = jnp.where(
            lax.broadcasted_iota(jnp.int32, (PATCH, nobs), 0) == cells_ref[p : p + 1, :], 1.0, 0.0
        )
        inverse_var = 1.0 / variance_ref[p : p + 1, :]
        pair = jnp.concatenate(
            [inverse_var, observed_ref[p : p + 1, :] * inverse_var, jnp.zeros((6, nobs), jnp.float32)],
            axis=0,
        )
        sums_ref[8 * p : 8 * (p + 1), :] = dot(pair, hot, NT)


def forecast_kernel(
    tiles, groups, prior_ref, vy_ref, vx_ref, dk_ref, order_ref,
    cells_ref, observed_ref, variance_ref, out_ref, sums_ref,
    below_ref, above_ref, below_c, above_c, hot_ref, parts_ref, outgoing, incoming,
    up_send, up_recv, down_send, down_recv, mem_send, mem_recv,
):
    tile, me = lax.axis_index("tile"), lax.axis_index("mem")
    members, height, width = prior_ref.shape
    group_columns = out_ref.shape[1]
    has_below, has_above = tile > 0, tile < tiles - 1
    enter(tile, tiles, me, groups)

    def halo(target, field, coefs, send, recv):
        pairs = [(prior_ref, field)] + [
            (ref, coefs.at[i]) for i, ref in enumerate((vy_ref, vx_ref, dk_ref))
        ]
        return [
            pltpu.make_async_remote_copy(
                src_ref=src, dst_ref=dst, send_sem=send.at[i], recv_sem=recv.at[i],
                device_id={"tile": target}, device_id_type=MESH,
            )
            for i, (src, dst) in enumerate(pairs)
        ]

    up = halo(tile + 1, below_ref, below_c, up_send, up_recv)
    down = halo(tile - 1, above_ref, above_c, down_send, down_recv)

    @pl.when(has_above)
    def _():
        for c in up:
            c.start()

    @pl.when(has_below)
    def _():
        for c in down:
            c.start()

    @pl.when(jnp.logical_not(has_below))
    def _():
        below_ref[...] = jnp.zeros_like(below_ref)
        below_c[...] = jnp.zeros_like(below_c)

    @pl.when(jnp.logical_not(has_above))
    def _():
        above_ref[...] = jnp.zeros_like(above_ref)
        above_c[...] = jnp.zeros_like(above_c)

    build_hot(order_ref, hot_ref)
    observation_sums(cells_ref, observed_ref, variance_ref, sums_ref)

    @pl.when(has_below)
    def _():
        for c in up:
            c.wait_recv()

    @pl.when(has_above)
    def _():
        for c in down:
            c.wait_recv()

    def slab(r):
        if r < 0:
            return below_ref[:, height + r, :]
        if r >= height:
            return above_ref[:, r - height, :]
        return prior_ref[:, r, :]

    def coefs(r):
        if r < 0:
            return [below_c[i, height + r : height + r + 1, :] for i in range(3)]
        if r >= height:
            return [above_c[i, r - height : r - height + 1, :] for i in range(3)]
        return [ref[r : r + 1, :] for ref in (vy_ref, vx_ref, dk_ref)]

    keep_below = jnp.where(has_below, 1.0, 0.0)
    keep_above = jnp.where(has_above, 1.0, 0.0)
    middle = {}
    for r in range(-2, height + 2):
        value = one_step([slab(r + o) for o in range(-2, 3)], *coefs(r))
        if r < 0:
            value = value * keep_below
        if r >= height:
            value = value * keep_above
        middle[r] = value
    for r in range(height):
        value = one_step([middle[r + o] for o in range(-2, 3)], *coefs(r))
        parts_ref[:, r * width : (r + 1) * width] = parts_of(value)

    sent = []
    order = sorted(range(1, groups), key=lambda k: abs(2 * k - groups))
    for k in order + [0]:
        target = lax.rem(me + k, groups)
        first = pl.multiple_of(target * group_columns, group_columns)
        block = picked(parts_ref[...], hot_ref[:, pl.ds(first, group_columns)])
        if k == 0:
            out_ref[pl.ds(pl.multiple_of(me * members, members), members), :] = block
            continue
        outgoing[k - 1] = block
        c = pltpu.make_async_remote_copy(
            src_ref=outgoing.at[k - 1], dst_ref=incoming.at[k - 1],
            send_sem=mem_send.at[k - 1], recv_sem=mem_recv.at[k - 1],
            device_id={"mem": target}, device_id_type=MESH,
        )
        c.start()
        sent.append((k, c))
    for k, c in reversed(sent):
        c.wait_recv()
        source = lax.rem(me - k + groups, groups)
        out_ref[pl.ds(pl.multiple_of(source * members, members), members), :] = incoming[k - 1]
    for k, c in sent:
        c.wait_send()

    @pl.when(has_above)
    def _():
        for c in up:
            c.wait_send()

    @pl.when(has_below)
    def _():
        for c in down:
            c.wait_send()


def return_kernel(
    tiles, groups, updated_ref, order_ref, out_ref,
    below_ref, above_ref, rows_ref, hot_ref, incoming,
    up_send, up_recv, down_send, down_recv, mem_send, mem_recv,
):
    tile, me = lax.axis_index("tile"), lax.axis_index("mem")
    extent, members, width = out_ref.shape
    height = extent - 4
    group_columns = updated_ref.shape[1]
    has_below, has_above = tile > 0, tile < tiles - 1
    enter(tile, tiles, me, groups)
    sent = []
    for k in sorted(range(1, groups), key=lambda k: abs(2 * k - groups)):
        target = lax.rem(me + k, groups)
        c = pltpu.make_async_remote_copy(
            src_ref=updated_ref.at[pl.ds(pl.multiple_of(target * members, members), members), :],
            dst_ref=incoming.at[k - 1],
            send_sem=mem_send.at[k - 1], recv_sem=mem_recv.at[k - 1],
            device_id={"mem": target}, device_id_type=MESH,
        )
        c.start()
        sent.append((k, c))
    build_inverse_hot(order_ref, hot_ref)
    up = pltpu.make_async_remote_copy(
        src_ref=rows_ref.at[pl.ds(height - 2, 2)], dst_ref=below_ref,
        send_sem=up_send, recv_sem=up_recv, device_id={"tile": tile + 1}, device_id_type=MESH,
    )
    down = pltpu.make_async_remote_copy(
        src_ref=rows_ref.at[pl.ds(0, 2)], dst_ref=above_ref,
        send_sem=down_send, recv_sem=down_recv, device_id={"tile": tile - 1}, device_id_type=MESH,
    )

    def share(source, value, r):
        first = pl.multiple_of(source * group_columns, group_columns)
        return picked(value, hot_ref[pl.ds(first, group_columns), r * width : (r + 1) * width])

    own = parts_of(updated_ref[pl.ds(pl.multiple_of(me * members, members), members), :])
    totals = [share(me, own, r) for r in range(height)]
    for k, c in list(reversed(sent)):
        c.wait_recv()
        source = lax.rem(me - k + groups, groups)
        value = parts_of(incoming[k - 1])
        last = k == sent[0][0]
        for r in range(height):
            totals[r] = totals[r] + share(source, value, r)
            if not last:
                continue
            rows_ref[r] = totals[r]
            if r == 1:

                @pl.when(has_below)
                def _():
                    down.start()

            if r == height - 1:

                @pl.when(has_above)
                def _():
                    up.start()

    for r in range(height):
        out_ref[r + 2] = totals[r]

    @pl.when(has_above)
    def _():
        down.wait_recv()

    @pl.when(has_below)
    def _():
        up.wait_recv()

    @pl.when(has_below)
    def _():
        out_ref[0:2] = below_ref[...]

    @pl.when(jnp.logical_not(has_below))
    def _():
        out_ref[0:2] = jnp.zeros_like(below_ref)

    @pl.when(has_above)
    def _():
        out_ref[height + 2 : height + 4] = above_ref[...]

    @pl.when(jnp.logical_not(has_above))
    def _():
        out_ref[height + 2 : height + 4] = jnp.zeros_like(above_ref)

    for k, c in sent:
        c.wait_send()

    @pl.when(has_below)
    def _():
        down.wait_send()

    @pl.when(has_above)
    def _():
        up.wait_send()


def last_kernel(rows_ref, vy_ref, vx_ref, dk_ref, out_ref):
    for r in range(out_ref.shape[1]):
        out_ref[:, r, :] = one_step(
            [rows_ref[r + o] for o in range(5)],
            *[ref[r : r + 1, :] for ref in (vy_ref, vx_ref, dk_ref)],
        )


def dot(a, b, dims=(((1,), (0,)), ((), ()))):
    return lax.dot_general(
        a, b, dims, precision=lax.Precision.HIGHEST, preferred_element_type=jnp.float32
    )


NT = (((1,), (1,)), ((), ()))


def analysis_kernel(members_ref, sums_ref, out_ref, system_ref, inverse_ref):
    size = members_ref.shape[0]
    patches = members_ref.shape[1] // PATCH
    floor = size - 1.0
    eye = jnp.where(
        lax.broadcasted_iota(jnp.int32, (size, size), 0)
        == lax.broadcasted_iota(jnp.int32, (size, size), 1),
        1.0,
        0.0,
    )
    spreads, centers, pulls, excess = [], [], [], []
    for p in range(patches):
        x = members_ref[:, p * PATCH : (p + 1) * PATCH]
        center = jnp.mean(x, axis=0, keepdims=True)
        spread = x - center
        d, w = sums_ref[8 * p : 8 * p + 1, :], sums_ref[8 * p + 1 : 8 * p + 2, :]
        gram = dot(spread * d, spread, NT)
        pulled = dot(jnp.broadcast_to(w - d * center, (8, PATCH)), spread, NT)
        bound = jnp.max(jnp.sum(jnp.abs(gram), axis=0, keepdims=True)) * 1.0001
        system = gram + floor * eye
        system_ref[p] = system
        scale = 2.0 / (2.0 * floor + bound)
        inverse_ref[p] = (2.0 * scale) * eye - (scale * scale) * system
        e = bound / floor
        spreads.append(spread)
        centers.append(center)
        pulls.append(pulled)
        excess.append(e * e / (4.0 * (1.0 + e)))

    def more(es):
        worst = es[0]
        for e in es[1:]:
            worst = jnp.maximum(worst, e)
        return worst > 1e-6

    def step(es):
        xs = [inverse_ref[p] for p in range(patches)]
        ms = [dot(xs[p], system_ref[p]) for p in range(patches)]
        ys = [dot(ms[p], xs[p]) for p in range(patches)]
        for p in range(patches):
            s = 2.0 * (1.0 + es[p]) / (2.0 + es[p])
            inverse_ref[p] = (2.0 * s) * xs[p] - (s * s) * ys[p]
        return tuple(e * e / (4.0 * (1.0 + e)) for e in es)

    lax.while_loop(more, step, tuple(excess))
    for p in range(patches):
        z = dot(inverse_ref[p], spreads[p])
        shift = dot(pulls[p], z)[0:1]
        out_ref[:, p * PATCH : (p + 1) * PATCH] = (
            centers[p] + shift + 0.5 * spreads[p] + (0.5 * floor) * z
        )


def analyze(members, sums):
    size = members.shape[0]
    patches = members.shape[1] // PATCH
    return pl.pallas_call(
        analysis_kernel,
        out_shape=jax.ShapeDtypeStruct(members.shape, jnp.float32),
        in_specs=[pl.BlockSpec(memory_space=pltpu.VMEM)] * 2,
        out_specs=pl.BlockSpec(memory_space=pltpu.VMEM),
        scratch_shapes=[
            pltpu.VMEM((patches, size, size), jnp.float32),
            pltpu.VMEM((patches, size, size), jnp.float32),
        ],
    )(members, sums)


def on_device(prior_ensemble_fields, vel_y, vel_x, diffus, assign, obs_cell, obs_value, obs_var):
    members, height, width = prior_ensemble_fields.shape
    columns = height * width
    tiles, groups = lax.axis_size("tile"), lax.axis_size("mem")
    group_columns = columns // groups
    vmem = pl.BlockSpec(memory_space=pltpu.VMEM)
    f32, bf16 = jnp.float32, jnp.bfloat16
    dma = pltpu.SemaphoreType.DMA
    patches = obs_cell.shape[0]
    gathered, sums = pl.pallas_call(
        functools.partial(forecast_kernel, tiles, groups),
        out_shape=(
            jax.ShapeDtypeStruct((members * groups, group_columns), f32),
            jax.ShapeDtypeStruct((8 * patches, PATCH), f32),
        ),
        in_specs=[vmem] * 8,
        out_specs=(vmem, vmem),
        scratch_shapes=[
            pltpu.VMEM((members, height, width), f32),
            pltpu.VMEM((members, height, width), f32),
            pltpu.VMEM((3, height, width), f32),
            pltpu.VMEM((3, height, width), f32),
            pltpu.VMEM((columns, columns), bf16),
            pltpu.VMEM((2 * members, columns), bf16),
            pltpu.VMEM((groups - 1, members, group_columns), f32),
            pltpu.VMEM((groups - 1, members, group_columns), f32),
            dma((4,)), dma((4,)), dma((4,)), dma((4,)), dma((groups - 1,)), dma((groups - 1,)),
        ],
        compiler_params=pltpu.CompilerParams(collective_id=0, has_side_effects=True),
    )(prior_ensemble_fields, vel_y, vel_x, diffus, assign, obs_cell, obs_value, obs_var)
    updated = analyze(gathered, sums)
    rows = pl.pallas_call(
        functools.partial(return_kernel, tiles, groups),
        out_shape=jax.ShapeDtypeStruct((height + 4, members, width), f32),
        in_specs=[vmem] * 2,
        out_specs=vmem,
        scratch_shapes=[
            pltpu.VMEM((2, members, width), f32),
            pltpu.VMEM((2, members, width), f32),
            pltpu.VMEM((height, members, width), f32),
            pltpu.VMEM((columns, columns), bf16),
            pltpu.VMEM((groups - 1, members, group_columns), f32),
            dma, dma, dma, dma, dma((groups - 1,)), dma((groups - 1,)),
        ],
        compiler_params=pltpu.CompilerParams(collective_id=1, has_side_effects=True),
    )(updated, assign)
    return pl.pallas_call(
        last_kernel,
        out_shape=jax.ShapeDtypeStruct((members, height, width), f32),
        in_specs=[vmem] * 4,
        out_specs=vmem,
    )(rows, vel_y, vel_x, diffus)


def solution(mesh):
    return jax.shard_map(
        on_device,
        mesh=mesh,
        in_specs=(
            P("mem", "tile", None),
            P("tile", None),
            P("tile", None),
            P("tile", None),
            P("tile", None),
            P(("tile", "mem"), None),
            P(("tile", "mem"), None),
            P(("tile", "mem"), None),
        ),
        out_specs=P("mem", "tile", None),
        check_vma=False,
    )
```

```python
import functools

import jax
import jax.numpy as jnp
from jax import lax
from jax.experimental import pallas as pl
from jax.experimental.pallas import tpu as pltpu
from jax.sharding import PartitionSpec as P

PATCH = 256


CHUNKS = 4
MESH = pl.DeviceIdType.MESH
NN = (((1,), (0,)), ((), ()))


def one_step(rows, coef_y, coef_x, coef_k):
    far_below, below, center, above, far_above = rows
    width = center.shape[1]
    grad_y = (far_below - far_above + 8.0 * (above - below)) * (1.0 / 12.0)
    right_one = pltpu.roll(center, width - 1, 1)
    left_one = pltpu.roll(center, 1, 1)
    right_two = pltpu.roll(center, width - 2, 1)
    left_two = pltpu.roll(center, 2, 1)
    grad_x = (left_two - right_two + 8.0 * (right_one - left_one)) * (1.0 / 12.0)
    lap = (above + below) + (right_one + left_one) - 4.0 * center
    return center - coef_y * grad_y - coef_x * grad_x + coef_k * lap


def enter(tile, tiles, me, groups, peers):
    barrier = pltpu.get_barrier_semaphore()
    for k in range(1, groups):
        pl.semaphore_signal(
            barrier, inc=1, device_id={"mem": lax.rem(me + k, groups)}, device_id_type=MESH
        )
    count = groups - 1
    for offset in peers:
        peer = tile + offset
        there = jnp.logical_and(peer >= 0, peer < tiles)
        count = count + jnp.where(there, 1, 0)

        @pl.when(there)
        def _():
            pl.semaphore_signal(barrier, inc=1, device_id={"tile": peer}, device_id_type=MESH)

    pl.semaphore_wait(barrier, count)


def build_hot(order_ref, hot_ref, part, count):
    columns = hot_ref.shape[0]
    block = 128

    def fill(i, carry):
        start = pl.multiple_of(i * block, block)
        row = lax.broadcasted_iota(jnp.int32, (block, columns), 0) + start
        hot_ref[pl.ds(start, block), :] = jnp.where(row == order_ref[...], 1.0, 0.0).astype(
            jnp.bfloat16
        )
        return carry

    steps = columns // block // count
    lax.fori_loop(part * steps, (part + 1) * steps, fill, 0)


def parts_of(value):
    high = value.astype(jnp.bfloat16)
    low = (value - high.astype(jnp.float32)).astype(jnp.bfloat16)
    return jnp.concatenate([high, low], axis=0)


def picked(parts, hot):
    wide = lax.dot_general(parts, hot, NN, preferred_element_type=jnp.float32)
    rows = wide.shape[0] // 2
    return wide[:rows] + wide[rows:]


def build_inverse_hot(order_ref, hot_ref):
    columns = hot_ref.shape[0]
    block = 128
    across = jnp.concatenate(
        [order_ref[:, i * block : (i + 1) * block] for i in range(columns // block)], axis=0
    )
    across = jnp.concatenate([across] * (block // across.shape[0]), axis=0)
    down = across.T
    place = lax.broadcasted_iota(jnp.int32, (block, columns), 1)
    for i in range(columns // block):
        hot_ref[i * block : (i + 1) * block, :] = jnp.where(
            place == down[:, i : i + 1], 1.0, 0.0
        ).astype(jnp.bfloat16)


def observation_sums(cells_ref, observed_ref, variance_ref, sums_ref):
    patches, nobs = cells_ref.shape
    for p in range(patches):
        hot = jnp.where(
            lax.broadcasted_iota(jnp.int32, (PATCH, nobs), 0) == cells_ref[p : p + 1, :], 1.0, 0.0
        )
        inverse_var = 1.0 / variance_ref[p : p + 1, :]
        pair = jnp.concatenate(
            [inverse_var, observed_ref[p : p + 1, :] * inverse_var, jnp.zeros((6, nobs), jnp.float32)],
            axis=0,
        )
        sums_ref[8 * p : 8 * (p + 1), :] = dot(pair, hot, NT)


def forecast_kernel(
    tiles, groups, prior_ref, vy_ref, vx_ref, dk_ref, order_ref,
    cells_ref, observed_ref, variance_ref, out_ref, sums_ref,
    near_ref, far_ref, near_c, far_c, hot_ref, parts_ref, outgoing, incoming,
    near_send, near_recv, far_send, far_recv, mem_send, mem_recv,
):
    tile, me = lax.axis_index("tile"), lax.axis_index("mem")
    members, height, width = prior_ref.shape
    group_columns = out_ref.shape[1]
    has_below, has_above = tile > 0, tile < tiles - 1
    odd = lax.rem(tile, 2)
    even = odd == 0
    partner = tile + 1 - 2 * odd
    onward = tile + 2 - 4 * odd
    behind = tile - 2 + 4 * odd
    passes = jnp.logical_and(onward >= 0, onward < tiles)
    has_far = jnp.logical_and(behind >= 0, behind < tiles)
    enter(tile, tiles, me, groups, (1 - 2 * odd, -2, 2))
    chunk = members // CHUNKS

    def hop(pairs, send, recv, target):
        return [
            pltpu.make_async_remote_copy(
                src_ref=src, dst_ref=dst, send_sem=send.at[i], recv_sem=recv.at[i],
                device_id={"tile": target}, device_id_type=MESH,
            )
            for i, (src, dst) in enumerate(pairs)
        ]

    cuts = [pl.ds(i * chunk, chunk) for i in range(CHUNKS)]
    first_hop = hop(
        [(prior_ref.at[cut], near_ref.at[cut]) for cut in cuts]
        + [(ref, near_c.at[i]) for i, ref in enumerate((vy_ref, vx_ref, dk_ref))],
        near_send, near_recv, partner,
    )
    second_hop = hop(
        [(near_ref.at[cut], far_ref.at[cut]) for cut in cuts]
        + [(near_c.at[i], far_c.at[i]) for i in range(3)],
        far_send, far_recv, onward,
    )
    for c in first_hop:
        c.start()

    @pl.when(jnp.logical_not(has_far))
    def _():
        far_ref[...] = jnp.zeros_like(far_ref)
        far_c[...] = jnp.zeros_like(far_c)

    for i in range(CHUNKS + 3):
        if i < CHUNKS:
            build_hot(order_ref, hot_ref, i, CHUNKS)
        first_hop[i].wait_recv()

        @pl.when(passes)
        def _():
            second_hop[i].start()

    observation_sums(cells_ref, observed_ref, variance_ref, sums_ref)

    @pl.when(has_far)
    def _():
        for c in second_hop:
            c.wait_recv()

    def slab(r):
        if r < 0:
            return jnp.where(even, far_ref[:, height + r, :], near_ref[:, height + r, :])
        if r >= height:
            return jnp.where(even, near_ref[:, r - height, :], far_ref[:, r - height, :])
        return prior_ref[:, r, :]

    def coefs(r):
        if r < 0:
            at = slice(height + r, height + r + 1)
            return [jnp.where(even, far_c[i, at, :], near_c[i, at, :]) for i in range(3)]
        if r >= height:
            at = slice(r - height, r - height + 1)
            return [jnp.where(even, near_c[i, at, :], far_c[i, at, :]) for i in range(3)]
        return [ref[r : r + 1, :] for ref in (vy_ref, vx_ref, dk_ref)]

    keep_below = jnp.where(has_below, 1.0, 0.0)
    keep_above = jnp.where(has_above, 1.0, 0.0)
    middle = {}
    for r in range(-2, height + 2):
        value = one_step([slab(r + o) for o in range(-2, 3)], *coefs(r))
        if r < 0:
            value = value * keep_below
        if r >= height:
            value = value * keep_above
        middle[r] = value
    for r in range(height):
        value = one_step([middle[r + o] for o in range(-2, 3)], *coefs(r))
        parts_ref[:, r * width : (r + 1) * width] = parts_of(value)

    sent = []
    order = sorted(range(1, groups), key=lambda k: abs(2 * k - groups))
    for k in order + [0]:
        target = lax.rem(me + k, groups)
        first = pl.multiple_of(target * group_columns, group_columns)
        block = picked(parts_ref[...], hot_ref[:, pl.ds(first, group_columns)])
        if k == 0:
            out_ref[pl.ds(pl.multiple_of(me * members, members), members), :] = block
            continue
        outgoing[k - 1] = block
        c = pltpu.make_async_remote_copy(
            src_ref=outgoing.at[k - 1], dst_ref=incoming.at[k - 1],
            send_sem=mem_send.at[k - 1], recv_sem=mem_recv.at[k - 1],
            device_id={"mem": target}, device_id_type=MESH,
        )
        c.start()
        sent.append((k, c))
    for k, c in reversed(sent):
        c.wait_recv()
        source = lax.rem(me - k + groups, groups)
        out_ref[pl.ds(pl.multiple_of(source * members, members), members), :] = incoming[k - 1]
    for k, c in sent:
        c.wait_send()

    for c in first_hop:
        c.wait_send()

    @pl.when(passes)
    def _():
        for c in second_hop:
            c.wait_send()


def return_kernel(
    tiles, groups, updated_ref, order_ref, out_ref,
    below_ref, above_ref, rows_ref, hot_ref, incoming,
    up_send, up_recv, down_send, down_recv, mem_send, mem_recv,
):
    tile, me = lax.axis_index("tile"), lax.axis_index("mem")
    extent, members, width = out_ref.shape
    height = extent - 4
    group_columns = updated_ref.shape[1]
    has_below, has_above = tile > 0, tile < tiles - 1
    enter(tile, tiles, me, groups, (-1, 1))
    sent = []
    for k in sorted(range(1, groups), key=lambda k: abs(2 * k - groups)):
        target = lax.rem(me + k, groups)
        c = pltpu.make_async_remote_copy(
            src_ref=updated_ref.at[pl.ds(pl.multiple_of(target * members, members), members), :],
            dst_ref=incoming.at[k - 1],
            send_sem=mem_send.at[k - 1], recv_sem=mem_recv.at[k - 1],
            device_id={"mem": target}, device_id_type=MESH,
        )
        c.start()
        sent.append((k, c))
    build_inverse_hot(order_ref, hot_ref)
    up = pltpu.make_async_remote_copy(
        src_ref=rows_ref.at[pl.ds(height - 2, 2)], dst_ref=below_ref,
        send_sem=up_send, recv_sem=up_recv, device_id={"tile": tile + 1}, device_id_type=MESH,
    )
    down = pltpu.make_async_remote_copy(
        src_ref=rows_ref.at[pl.ds(0, 2)], dst_ref=above_ref,
        send_sem=down_send, recv_sem=down_recv, device_id={"tile": tile - 1}, device_id_type=MESH,
    )

    def share(source, value, r):
        first = pl.multiple_of(source * group_columns, group_columns)
        return picked(value, hot_ref[pl.ds(first, group_columns), r * width : (r + 1) * width])

    own = parts_of(updated_ref[pl.ds(pl.multiple_of(me * members, members), members), :])
    totals = [share(me, own, r) for r in range(height)]
    for k, c in list(reversed(sent)):
        c.wait_recv()
        source = lax.rem(me - k + groups, groups)
        value = parts_of(incoming[k - 1])
        last = k == sent[0][0]
        for r in range(height):
            totals[r] = totals[r] + share(source, value, r)
            if not last:
                continue
            rows_ref[r] = totals[r]
            if r == 1:

                @pl.when(has_below)
                def _():
                    down.start()

            if r == height - 1:

                @pl.when(has_above)
                def _():
                    up.start()

    for r in range(height):
        out_ref[r + 2] = totals[r]

    @pl.when(has_above)
    def _():
        down.wait_recv()

    @pl.when(has_below)
    def _():
        up.wait_recv()

    @pl.when(has_below)
    def _():
        out_ref[0:2] = below_ref[...]

    @pl.when(jnp.logical_not(has_below))
    def _():
        out_ref[0:2] = jnp.zeros_like(below_ref)

    @pl.when(has_above)
    def _():
        out_ref[height + 2 : height + 4] = above_ref[...]

    @pl.when(jnp.logical_not(has_above))
    def _():
        out_ref[height + 2 : height + 4] = jnp.zeros_like(above_ref)

    for k, c in sent:
        c.wait_send()

    @pl.when(has_below)
    def _():
        down.wait_send()

    @pl.when(has_above)
    def _():
        up.wait_send()


def last_kernel(rows_ref, vy_ref, vx_ref, dk_ref, out_ref):
    for r in range(out_ref.shape[1]):
        out_ref[:, r, :] = one_step(
            [rows_ref[r + o] for o in range(5)],
            *[ref[r : r + 1, :] for ref in (vy_ref, vx_ref, dk_ref)],
        )


def dot(a, b, dims=(((1,), (0,)), ((), ()))):
    return lax.dot_general(
        a, b, dims, precision=lax.Precision.HIGHEST, preferred_element_type=jnp.float32
    )


NT = (((1,), (1,)), ((), ()))


def analysis_kernel(members_ref, sums_ref, out_ref, system_ref, inverse_ref):
    size = members_ref.shape[0]
    patches = members_ref.shape[1] // PATCH
    floor = size - 1.0
    eye = jnp.where(
        lax.broadcasted_iota(jnp.int32, (size, size), 0)
        == lax.broadcasted_iota(jnp.int32, (size, size), 1),
        1.0,
        0.0,
    )
    spreads, centers, pulls, excess = [], [], [], []
    for p in range(patches):
        x = members_ref[:, p * PATCH : (p + 1) * PATCH]
        center = jnp.mean(x, axis=0, keepdims=True)
        spread = x - center
        d, w = sums_ref[8 * p : 8 * p + 1, :], sums_ref[8 * p + 1 : 8 * p + 2, :]
        gram = dot(spread * d, spread, NT)
        pulled = dot(jnp.broadcast_to(w - d * center, (8, PATCH)), spread, NT)
        bound = jnp.max(jnp.sum(jnp.abs(gram), axis=0, keepdims=True)) * 1.0001
        system = gram + floor * eye
        system_ref[p] = system
        scale = 2.0 / (2.0 * floor + bound)
        inverse_ref[p] = (2.0 * scale) * eye - (scale * scale) * system
        e = bound / floor
        spreads.append(spread)
        centers.append(center)
        pulls.append(pulled)
        excess.append(e * e / (4.0 * (1.0 + e)))

    def more(es):
        worst = es[0]
        for e in es[1:]:
            worst = jnp.maximum(worst, e)
        return worst > 1e-6

    def step(es):
        xs = [inverse_ref[p] for p in range(patches)]
        ms = [dot(xs[p], system_ref[p]) for p in range(patches)]
        ys = [dot(ms[p], xs[p]) for p in range(patches)]
        for p in range(patches):
            s = 2.0 * (1.0 + es[p]) / (2.0 + es[p])
            inverse_ref[p] = (2.0 * s) * xs[p] - (s * s) * ys[p]
        return tuple(e * e / (4.0 * (1.0 + e)) for e in es)

    lax.while_loop(more, step, tuple(excess))
    for p in range(patches):
        z = dot(inverse_ref[p], spreads[p])
        shift = dot(pulls[p], z)[0:1]
        out_ref[:, p * PATCH : (p + 1) * PATCH] = (
            centers[p] + shift + 0.5 * spreads[p] + (0.5 * floor) * z
        )


def analyze(members, sums):
    size = members.shape[0]
    patches = members.shape[1] // PATCH
    return pl.pallas_call(
        analysis_kernel,
        out_shape=jax.ShapeDtypeStruct(members.shape, jnp.float32),
        in_specs=[pl.BlockSpec(memory_space=pltpu.VMEM)] * 2,
        out_specs=pl.BlockSpec(memory_space=pltpu.VMEM),
        scratch_shapes=[
            pltpu.VMEM((patches, size, size), jnp.float32),
            pltpu.VMEM((patches, size, size), jnp.float32),
        ],
    )(members, sums)


def on_device(prior_ensemble_fields, vel_y, vel_x, diffus, assign, obs_cell, obs_value, obs_var):
    members, height, width = prior_ensemble_fields.shape
    columns = height * width
    tiles, groups = lax.axis_size("tile"), lax.axis_size("mem")
    group_columns = columns // groups
    vmem = pl.BlockSpec(memory_space=pltpu.VMEM)
    f32, bf16 = jnp.float32, jnp.bfloat16
    dma = pltpu.SemaphoreType.DMA
    patches = obs_cell.shape[0]
    gathered, sums = pl.pallas_call(
        functools.partial(forecast_kernel, tiles, groups),
        out_shape=(
            jax.ShapeDtypeStruct((members * groups, group_columns), f32),
            jax.ShapeDtypeStruct((8 * patches, PATCH), f32),
        ),
        in_specs=[vmem] * 8,
        out_specs=(vmem, vmem),
        scratch_shapes=[
            pltpu.VMEM((members, height, width), f32),
            pltpu.VMEM((members, height, width), f32),
            pltpu.VMEM((3, height, width), f32),
            pltpu.VMEM((3, height, width), f32),
            pltpu.VMEM((columns, columns), bf16),
            pltpu.VMEM((2 * members, columns), bf16),
            pltpu.VMEM((groups - 1, members, group_columns), f32),
            pltpu.VMEM((groups - 1, members, group_columns), f32),
            *[dma((CHUNKS + 3,))] * 4, dma((groups - 1,)), dma((groups - 1,)),
        ],
        compiler_params=pltpu.CompilerParams(collective_id=0, has_side_effects=True),
    )(prior_ensemble_fields, vel_y, vel_x, diffus, assign, obs_cell, obs_value, obs_var)
    updated = analyze(gathered, sums)
    rows = pl.pallas_call(
        functools.partial(return_kernel, tiles, groups),
        out_shape=jax.ShapeDtypeStruct((height + 4, members, width), f32),
        in_specs=[vmem] * 2,
        out_specs=vmem,
        scratch_shapes=[
            pltpu.VMEM((2, members, width), f32),
            pltpu.VMEM((2, members, width), f32),
            pltpu.VMEM((height, members, width), f32),
            pltpu.VMEM((columns, columns), bf16),
            pltpu.VMEM((groups - 1, members, group_columns), f32),
            dma, dma, dma, dma, dma((groups - 1,)), dma((groups - 1,)),
        ],
        compiler_params=pltpu.CompilerParams(collective_id=1, has_side_effects=True),
    )(updated, assign)
    return pl.pallas_call(
        last_kernel,
        out_shape=jax.ShapeDtypeStruct((members, height, width), f32),
        in_specs=[vmem] * 4,
        out_specs=vmem,
    )(rows, vel_y, vel_x, diffus)


def solution(mesh):
    return jax.shard_map(
        on_device,
        mesh=mesh,
        in_specs=(
            P("mem", "tile", None),
            P("tile", None),
            P("tile", None),
            P("tile", None),
            P("tile", None),
            P(("tile", "mem"), None),
            P(("tile", "mem"), None),
            P(("tile", "mem"), None),
        ),
        out_specs=P("mem", "tile", None),
        check_vma=False,
    )
```

```python
import functools

import jax
import jax.numpy as jnp
from jax import lax
from jax.experimental import pallas as pl
from jax.experimental.pallas import tpu as pltpu
from jax.sharding import PartitionSpec as P

PATCH = 256


CHUNKS = 8
MESH = pl.DeviceIdType.MESH
NN = (((1,), (0,)), ((), ()))


def one_step(rows, coef_y, coef_x, coef_k):
    far_below, below, center, above, far_above = rows
    width = center.shape[1]
    grad_y = (far_below - far_above + 8.0 * (above - below)) * (1.0 / 12.0)
    right_one = pltpu.roll(center, width - 1, 1)
    left_one = pltpu.roll(center, 1, 1)
    right_two = pltpu.roll(center, width - 2, 1)
    left_two = pltpu.roll(center, 2, 1)
    grad_x = (left_two - right_two + 8.0 * (right_one - left_one)) * (1.0 / 12.0)
    lap = (above + below) + (right_one + left_one) - 4.0 * center
    return center - coef_y * grad_y - coef_x * grad_x + coef_k * lap


def enter(tile, tiles, me, groups, peers):
    barrier = pltpu.get_barrier_semaphore()
    for k in range(1, groups):
        pl.semaphore_signal(
            barrier, inc=1, device_id={"mem": lax.rem(me + k, groups)}, device_id_type=MESH
        )
    count = groups - 1
    for offset in peers:
        peer = tile + offset
        there = jnp.logical_and(peer >= 0, peer < tiles)
        count = count + jnp.where(there, 1, 0)

        @pl.when(there)
        def _():
            pl.semaphore_signal(barrier, inc=1, device_id={"tile": peer}, device_id_type=MESH)

    pl.semaphore_wait(barrier, count)


def build_hot(order_ref, hot_ref, part, count):
    columns = hot_ref.shape[0]
    block = 128

    def fill(i, carry):
        start = pl.multiple_of(i * block, block)
        row = lax.broadcasted_iota(jnp.int32, (block, columns), 0) + start
        hot_ref[pl.ds(start, block), :] = jnp.where(row == order_ref[...], 1.0, 0.0).astype(
            jnp.bfloat16
        )
        return carry

    steps = columns // block // count
    lax.fori_loop(part * steps, (part + 1) * steps, fill, 0)


def parts_of(value):
    high = value.astype(jnp.bfloat16)
    low = (value - high.astype(jnp.float32)).astype(jnp.bfloat16)
    return jnp.concatenate([high, low], axis=0)


def picked(parts, hot):
    wide = lax.dot_general(parts, hot, NN, preferred_element_type=jnp.float32)
    rows = wide.shape[0] // 2
    return wide[:rows] + wide[rows:]


def build_inverse_hot(order_ref, hot_ref):
    columns = hot_ref.shape[0]
    block = 128
    across = jnp.concatenate(
        [order_ref[:, i * block : (i + 1) * block] for i in range(columns // block)], axis=0
    )
    across = jnp.concatenate([across] * (block // across.shape[0]), axis=0)
    down = across.T
    place = lax.broadcasted_iota(jnp.int32, (block, columns), 1)
    for i in range(columns // block):
        hot_ref[i * block : (i + 1) * block, :] = jnp.where(
            place == down[:, i : i + 1], 1.0, 0.0
        ).astype(jnp.bfloat16)


def observation_sums(cells_ref, observed_ref, variance_ref, sums_ref):
    patches, nobs = cells_ref.shape
    for p in range(patches):
        hot = jnp.where(
            lax.broadcasted_iota(jnp.int32, (PATCH, nobs), 0) == cells_ref[p : p + 1, :], 1.0, 0.0
        )
        inverse_var = 1.0 / variance_ref[p : p + 1, :]
        pair = jnp.concatenate(
            [inverse_var, observed_ref[p : p + 1, :] * inverse_var, jnp.zeros((6, nobs), jnp.float32)],
            axis=0,
        )
        sums_ref[8 * p : 8 * (p + 1), :] = dot(pair, hot, NT)


def forecast_kernel(
    tiles, groups, prior_ref, vy_ref, vx_ref, dk_ref, order_ref,
    cells_ref, observed_ref, variance_ref, out_ref, sums_ref,
    near_ref, far_ref, near_c, far_c, hot_ref, parts_ref, outgoing, incoming,
    near_send, near_recv, far_send, far_recv, mem_send, mem_recv,
):
    tile, me = lax.axis_index("tile"), lax.axis_index("mem")
    members, height, width = prior_ref.shape
    group_columns = out_ref.shape[1]
    has_below, has_above = tile > 0, tile < tiles - 1
    odd = lax.rem(tile, 2)
    even = odd == 0
    partner = tile + 1 - 2 * odd
    onward = tile + 2 - 4 * odd
    behind = tile - 2 + 4 * odd
    passes = jnp.logical_and(onward >= 0, onward < tiles)
    has_far = jnp.logical_and(behind >= 0, behind < tiles)
    enter(tile, tiles, me, groups, (1 - 2 * odd, -2, 2))
    chunk = members // CHUNKS

    def hop(pairs, send, recv, target):
        return [
            pltpu.make_async_remote_copy(
                src_ref=src, dst_ref=dst, send_sem=send.at[i], recv_sem=recv.at[i],
                device_id={"tile": target}, device_id_type=MESH,
            )
            for i, (src, dst) in enumerate(pairs)
        ]

    cuts = [pl.ds(i * chunk, chunk) for i in range(CHUNKS)]
    first_hop = hop(
        [(prior_ref.at[cut], near_ref.at[cut]) for cut in cuts]
        + [(ref, near_c.at[i]) for i, ref in enumerate((vy_ref, vx_ref, dk_ref))],
        near_send, near_recv, partner,
    )
    second_hop = hop(
        [(near_ref.at[cut], far_ref.at[cut]) for cut in cuts]
        + [(near_c.at[i], far_c.at[i]) for i in range(3)],
        far_send, far_recv, onward,
    )
    for c in first_hop:
        c.start()

    @pl.when(jnp.logical_not(has_far))
    def _():
        far_ref[...] = jnp.zeros_like(far_ref)
        far_c[...] = jnp.zeros_like(far_c)

    for i in range(CHUNKS + 3):
        if i < CHUNKS:
            build_hot(order_ref, hot_ref, i, CHUNKS)
        first_hop[i].wait_recv()

        @pl.when(passes)
        def _():
            second_hop[i].start()

    observation_sums(cells_ref, observed_ref, variance_ref, sums_ref)

    @pl.when(has_far)
    def _():
        for c in second_hop:
            c.wait_recv()

    def slab(r):
        if r < 0:
            return jnp.where(even, far_ref[:, height + r, :], near_ref[:, height + r, :])
        if r >= height:
            return jnp.where(even, near_ref[:, r - height, :], far_ref[:, r - height, :])
        return prior_ref[:, r, :]

    def coefs(r):
        if r < 0:
            at = slice(height + r, height + r + 1)
            return [jnp.where(even, far_c[i, at, :], near_c[i, at, :]) for i in range(3)]
        if r >= height:
            at = slice(r - height, r - height + 1)
            return [jnp.where(even, near_c[i, at, :], far_c[i, at, :]) for i in range(3)]
        return [ref[r : r + 1, :] for ref in (vy_ref, vx_ref, dk_ref)]

    keep_below = jnp.where(has_below, 1.0, 0.0)
    keep_above = jnp.where(has_above, 1.0, 0.0)
    middle = {}
    for r in range(-2, height + 2):
        value = one_step([slab(r + o) for o in range(-2, 3)], *coefs(r))
        if r < 0:
            value = value * keep_below
        if r >= height:
            value = value * keep_above
        middle[r] = value
    for r in range(height):
        value = one_step([middle[r + o] for o in range(-2, 3)], *coefs(r))
        parts_ref[:, r * width : (r + 1) * width] = parts_of(value)

    sent = []
    order = sorted(range(1, groups), key=lambda k: abs(2 * k - groups))
    for k in order + [0]:
        target = lax.rem(me + k, groups)
        first = pl.multiple_of(target * group_columns, group_columns)
        block = picked(parts_ref[...], hot_ref[:, pl.ds(first, group_columns)])
        if k == 0:
            out_ref[pl.ds(pl.multiple_of(me * members, members), members), :] = block
            continue
        outgoing[k - 1] = block
        c = pltpu.make_async_remote_copy(
            src_ref=outgoing.at[k - 1], dst_ref=incoming.at[k - 1],
            send_sem=mem_send.at[k - 1], recv_sem=mem_recv.at[k - 1],
            device_id={"mem": target}, device_id_type=MESH,
        )
        c.start()
        sent.append((k, c))
    for k, c in reversed(sent):
        c.wait_recv()
        source = lax.rem(me - k + groups, groups)
        out_ref[pl.ds(pl.multiple_of(source * members, members), members), :] = incoming[k - 1]
    for k, c in sent:
        c.wait_send()

    for c in first_hop:
        c.wait_send()

    @pl.when(passes)
    def _():
        for c in second_hop:
            c.wait_send()


def return_kernel(
    tiles, groups, updated_ref, order_ref, out_ref,
    below_ref, above_ref, rows_ref, hot_ref, incoming,
    up_send, up_recv, down_send, down_recv, mem_send, mem_recv,
):
    tile, me = lax.axis_index("tile"), lax.axis_index("mem")
    extent, members, width = out_ref.shape
    height = extent - 4
    group_columns = updated_ref.shape[1]
    has_below, has_above = tile > 0, tile < tiles - 1
    enter(tile, tiles, me, groups, (-1, 1))
    sent = []
    for k in sorted(range(1, groups), key=lambda k: abs(2 * k - groups)):
        target = lax.rem(me + k, groups)
        c = pltpu.make_async_remote_copy(
            src_ref=updated_ref.at[pl.ds(pl.multiple_of(target * members, members), members), :],
            dst_ref=incoming.at[k - 1],
            send_sem=mem_send.at[k - 1], recv_sem=mem_recv.at[k - 1],
            device_id={"mem": target}, device_id_type=MESH,
        )
        c.start()
        sent.append((k, c))
    build_inverse_hot(order_ref, hot_ref)
    up = pltpu.make_async_remote_copy(
        src_ref=rows_ref.at[pl.ds(height - 2, 2)], dst_ref=below_ref,
        send_sem=up_send, recv_sem=up_recv, device_id={"tile": tile + 1}, device_id_type=MESH,
    )
    down = pltpu.make_async_remote_copy(
        src_ref=rows_ref.at[pl.ds(0, 2)], dst_ref=above_ref,
        send_sem=down_send, recv_sem=down_recv, device_id={"tile": tile - 1}, device_id_type=MESH,
    )

    def share(source, value, r):
        first = pl.multiple_of(source * group_columns, group_columns)
        return picked(value, hot_ref[pl.ds(first, group_columns), r * width : (r + 1) * width])

    own = parts_of(updated_ref[pl.ds(pl.multiple_of(me * members, members), members), :])
    totals = [share(me, own, r) for r in range(height)]
    for k, c in list(reversed(sent)):
        c.wait_recv()
        source = lax.rem(me - k + groups, groups)
        value = parts_of(incoming[k - 1])
        last = k == sent[0][0]
        for r in range(height):
            totals[r] = totals[r] + share(source, value, r)
            if not last:
                continue
            rows_ref[r] = totals[r]
            if r == 1:

                @pl.when(has_below)
                def _():
                    down.start()

            if r == height - 1:

                @pl.when(has_above)
                def _():
                    up.start()

    for r in range(height):
        out_ref[r + 2] = totals[r]

    @pl.when(has_above)
    def _():
        down.wait_recv()

    @pl.when(has_below)
    def _():
        up.wait_recv()

    @pl.when(has_below)
    def _():
        out_ref[0:2] = below_ref[...]

    @pl.when(jnp.logical_not(has_below))
    def _():
        out_ref[0:2] = jnp.zeros_like(below_ref)

    @pl.when(has_above)
    def _():
        out_ref[height + 2 : height + 4] = above_ref[...]

    @pl.when(jnp.logical_not(has_above))
    def _():
        out_ref[height + 2 : height + 4] = jnp.zeros_like(above_ref)

    for k, c in sent:
        c.wait_send()

    @pl.when(has_below)
    def _():
        down.wait_send()

    @pl.when(has_above)
    def _():
        up.wait_send()


def last_kernel(rows_ref, vy_ref, vx_ref, dk_ref, out_ref):
    for r in range(out_ref.shape[1]):
        out_ref[:, r, :] = one_step(
            [rows_ref[r + o] for o in range(5)],
            *[ref[r : r + 1, :] for ref in (vy_ref, vx_ref, dk_ref)],
        )


def dot(a, b, dims=(((1,), (0,)), ((), ()))):
    return lax.dot_general(
        a, b, dims, precision=lax.Precision.HIGHEST, preferred_element_type=jnp.float32
    )


NT = (((1,), (1,)), ((), ()))


def analysis_kernel(members_ref, sums_ref, out_ref, system_ref, inverse_ref):
    size = members_ref.shape[0]
    patches = members_ref.shape[1] // PATCH
    floor = size - 1.0
    eye = jnp.where(
        lax.broadcasted_iota(jnp.int32, (size, size), 0)
        == lax.broadcasted_iota(jnp.int32, (size, size), 1),
        1.0,
        0.0,
    )
    spreads, centers, pulls, excess = [], [], [], []
    for p in range(patches):
        x = members_ref[:, p * PATCH : (p + 1) * PATCH]
        center = jnp.mean(x, axis=0, keepdims=True)
        spread = x - center
        d, w = sums_ref[8 * p : 8 * p + 1, :], sums_ref[8 * p + 1 : 8 * p + 2, :]
        gram = dot(spread * d, spread, NT)
        pulled = dot(jnp.broadcast_to(w - d * center, (8, PATCH)), spread, NT)
        bound = jnp.max(jnp.sum(jnp.abs(gram), axis=0, keepdims=True)) * 1.0001
        system = gram + floor * eye
        system_ref[p] = system
        scale = 2.0 / (2.0 * floor + bound)
        inverse_ref[p] = (2.0 * scale) * eye - (scale * scale) * system
        e = bound / floor
        spreads.append(spread)
        centers.append(center)
        pulls.append(pulled)
        excess.append(e * e / (4.0 * (1.0 + e)))

    def more(es):
        worst = es[0]
        for e in es[1:]:
            worst = jnp.maximum(worst, e)
        return worst > 1e-6

    def step(es):
        xs = [inverse_ref[p] for p in range(patches)]
        ms = [dot(xs[p], system_ref[p]) for p in range(patches)]
        ys = [dot(ms[p], xs[p]) for p in range(patches)]
        for p in range(patches):
            s = 2.0 * (1.0 + es[p]) / (2.0 + es[p])
            inverse_ref[p] = (2.0 * s) * xs[p] - (s * s) * ys[p]
        return tuple(e * e / (4.0 * (1.0 + e)) for e in es)

    lax.while_loop(more, step, tuple(excess))
    for p in range(patches):
        z = dot(inverse_ref[p], spreads[p])
        shift = dot(pulls[p], z)[0:1]
        out_ref[:, p * PATCH : (p + 1) * PATCH] = (
            centers[p] + shift + 0.5 * spreads[p] + (0.5 * floor) * z
        )


def analyze(members, sums):
    size = members.shape[0]
    patches = members.shape[1] // PATCH
    return pl.pallas_call(
        analysis_kernel,
        out_shape=jax.ShapeDtypeStruct(members.shape, jnp.float32),
        in_specs=[pl.BlockSpec(memory_space=pltpu.VMEM)] * 2,
        out_specs=pl.BlockSpec(memory_space=pltpu.VMEM),
        scratch_shapes=[
            pltpu.VMEM((patches, size, size), jnp.float32),
            pltpu.VMEM((patches, size, size), jnp.float32),
        ],
    )(members, sums)


def on_device(prior_ensemble_fields, vel_y, vel_x, diffus, assign, obs_cell, obs_value, obs_var):
    members, height, width = prior_ensemble_fields.shape
    columns = height * width
    tiles, groups = lax.axis_size("tile"), lax.axis_size("mem")
    group_columns = columns // groups
    vmem = pl.BlockSpec(memory_space=pltpu.VMEM)
    f32, bf16 = jnp.float32, jnp.bfloat16
    dma = pltpu.SemaphoreType.DMA
    patches = obs_cell.shape[0]
    gathered, sums = pl.pallas_call(
        functools.partial(forecast_kernel, tiles, groups),
        out_shape=(
            jax.ShapeDtypeStruct((members * groups, group_columns), f32),
            jax.ShapeDtypeStruct((8 * patches, PATCH), f32),
        ),
        in_specs=[vmem] * 8,
        out_specs=(vmem, vmem),
        scratch_shapes=[
            pltpu.VMEM((members, height, width), f32),
            pltpu.VMEM((members, height, width), f32),
            pltpu.VMEM((3, height, width), f32),
            pltpu.VMEM((3, height, width), f32),
            pltpu.VMEM((columns, columns), bf16),
            pltpu.VMEM((2 * members, columns), bf16),
            pltpu.VMEM((groups - 1, members, group_columns), f32),
            pltpu.VMEM((groups - 1, members, group_columns), f32),
            *[dma((CHUNKS + 3,))] * 4, dma((groups - 1,)), dma((groups - 1,)),
        ],
        compiler_params=pltpu.CompilerParams(collective_id=0, has_side_effects=True),
    )(prior_ensemble_fields, vel_y, vel_x, diffus, assign, obs_cell, obs_value, obs_var)
    updated = analyze(gathered, sums)
    rows = pl.pallas_call(
        functools.partial(return_kernel, tiles, groups),
        out_shape=jax.ShapeDtypeStruct((height + 4, members, width), f32),
        in_specs=[vmem] * 2,
        out_specs=vmem,
        scratch_shapes=[
            pltpu.VMEM((2, members, width), f32),
            pltpu.VMEM((2, members, width), f32),
            pltpu.VMEM((height, members, width), f32),
            pltpu.VMEM((columns, columns), bf16),
            pltpu.VMEM((groups - 1, members, group_columns), f32),
            dma, dma, dma, dma, dma((groups - 1,)), dma((groups - 1,)),
        ],
        compiler_params=pltpu.CompilerParams(collective_id=1, has_side_effects=True),
    )(updated, assign)
    return pl.pallas_call(
        last_kernel,
        out_shape=jax.ShapeDtypeStruct((members, height, width), f32),
        in_specs=[vmem] * 4,
        out_specs=vmem,
    )(rows, vel_y, vel_x, diffus)


def solution(mesh):
    return jax.shard_map(
        on_device,
        mesh=mesh,
        in_specs=(
            P("mem", "tile", None),
            P("tile", None),
            P("tile", None),
            P("tile", None),
            P("tile", None),
            P(("tile", "mem"), None),
            P(("tile", "mem"), None),
            P(("tile", "mem"), None),
        ),
        out_specs=P("mem", "tile", None),
        check_vma=False,
    )
```
